32 devices in a mesh: dp: 16 (over z, x, core), tensor: 2 (over y).
Axes of the slice: x: 2, y: 2, z: 4, core: 2. Of those that a mesh axis runs over, the one named last changes fastest.
Arguments:
- block_input: float32 [4096, 1024], P(('dp', 'tensor')), may hold values from -6 to 6
- output_cotangent: float32 [4096, 1024], P(('dp', 'tensor')), may hold values from -6 to 6
- sequence_lengths: int32 [16, 4], P('dp'), may hold values from 1 to 128, 256 in all within a row
- first_gain: bfloat16 [1024], P('dp'), may hold values from 0.5 to 1.5
- first_shift: bfloat16 [1024], P('dp'), may hold values from -1.796875 to 1.796875
- heads_weight: bfloat16 [3, 1024, 1024], P(None, 'dp', 'tensor'), may hold values from -0.1875 to 0.1875
- heads_bias: bfloat16 [3, 1024], P(None, ('tensor', 'dp')), may hold values from -1.796875 to 1.796875
- mixer_weight: bfloat16 [1024, 1024], P('tensor', 'dp'), may hold values from -0.75 to 0.75
- mixer_bias: bfloat16 [1024], P('dp'), may hold values from -1.796875 to 1.796875
- second_gain: bfloat16 [1024], P('dp'), may hold values from 0.5 to 1.5
- second_shift: bfloat16 [1024], P('dp'), may hold values from -1.796875 to 1.796875
- widen_weight: bfloat16 [1024, 4096], P('dp', 'tensor'), may hold values from -0.1875 to 0.1875
- widen_bias: bfloat16 [4096], P(('tensor', 'dp')), may hold values from -1.796875 to 1.796875
- narrow_weight: bfloat16 [4096, 1024], P('tensor', 'dp'), may hold values from -0.09375 to 0.09375
- narrow_bias: bfloat16 [1024], P('dp'), may hold values from -1.796875 to 1.796875
Outputs:
- block_output: float32 [4096, 1024], P(('dp', 'tensor'))
- input_gradient: float32 [4096, 1024], P(('dp', 'tensor'))
- first_gain_gradient: float32 [1024], P(('dp', 'tensor'))
- first_shift_gradient: float32 [1024], P(('dp', 'tensor'))
- heads_weight_gradient: float32 [3, 1024, 1024], P(None, 'dp', 'tensor')
- heads_bias_gradient: float32 [3, 1024], P(None, ('tensor', 'dp'))
- mixer_weight_gradient: float32 [1024, 1024], P('tensor', 'dp')
- mixer_bias_gradient: float32 [1024], P(('dp', 'tensor'))
- second_gain_gradient: float32 [1024], P(('dp', 'tensor'))
- second_shift_gradient: float32 [1024], P(('dp', 'tensor'))
- widen_weight_gradient: float32 [1024, 4096], P('dp', 'tensor')
- widen_bias_gradient: float32 [4096], P(('tensor', 'dp'))
- narrow_weight_gradient: float32 [4096, 1024], P('tensor', 'dp')
- narrow_bias_gradient: float32 [1024], P(('dp', 'tensor'))
The draws below stay inside these ranges and needn't reach their ends.
Inputs may be any that keep to these rules, and one draw needn't show every extreme that they name: `sequence_lengths`: each row holds the lengths of one data shard's sequences, in order, summing to 256.
All inputs are finite; a program needn't handle non-finite values.
Results may differ from the reference program's by a relative error of at most 0.015.
Values may be sent and summed in bfloat16 or wider, within the bound.
No kernel may reach another device: no remote copies, remote signals or barrier semaphores. Data moves between devices by JAX's collectives and lax.ppermute only.
A program may use at most 128 MiB of HBM per device.

```python
import math
import jax
import jax.numpy as jnp
import numpy as np
from jax import lax

D = 1024
H = 16
HD = 64
FF = 4096
TOK_DEV = 256
SEQS = 4
MOST = 128
TOKENS = 4096
N_DP = 16


def spiked(values, stream_key, source, target, parts, factor):
    owner, partner = [(jnp.arange(values.shape[position]) // (values.shape[position] // parts)).reshape([-1 if axis == position else 1 for axis in range(values.ndim)]) for position in (source, target)]
    chosen = jax.random.permutation(stream_key, parts)[partner]
    strong = (owner == chosen) | (owner == (partner + parts // 2) % parts)
    return jnp.where(strong, factor * values, values)


def level_of(stream_key, shape, split, least, high):
    level, own = 1.0, jax.random.fold_in(stream_key, 6)
    for axis_at, blocks in split:
        heights = jnp.exp(jax.random.uniform(jax.random.fold_in(own, axis_at), (blocks,), jnp.float32, least / len(split), high / len(split)))
        level = level * jnp.repeat(heights, shape[axis_at] // blocks).reshape([-1 if axis == axis_at else 1 for axis in range(len(shape))])
    return level


def profile(amount, total, reach, skew):
    weights = [(1 << 20) // math.isqrt(grade ** skew) + 1 for grade in range(2, amount + 1)]
    spare, counts = total - reach - (amount - 1), [1] * (amount - 1)
    while spare > 0:
        candidates = [i for i in range(amount - 1) if counts[i] < reach]
        pool, left = sum([weights[i] for i in candidates]), spare
        for i in candidates:
            addition = min(reach - counts[i], max(1, left * weights[i] // pool), spare)
            counts[i] = counts[i] + addition
            spare = spare - addition
    return np.array([reach] + counts)


def ragged_sizes(own_key, number_of, total, most, lean):
    if number_of == 2:
        one = jax.random.randint(own_key, (), max(1, total - most), min(most, total - 1) + 1)
        return jnp.stack([one, total - one])
    tallies = jnp.asarray(profile(number_of, total, most, lean), jnp.int32)
    pairs = (number_of - 1) // 2
    giver, sink = tallies[1:1 + 2 * pairs:2], tallies[2:2 + 2 * pairs:2]
    margin = jnp.minimum(giver - 1, most - sink)
    passed = jax.random.randint(jax.random.fold_in(own_key, 1), (pairs,), 0, 1 << 20) % (margin + 1)
    tallies = tallies.at[1:1 + 2 * pairs:2].set(giver - passed).at[2:2 + 2 * pairs:2].set(sink + passed)
    return tallies[jax.random.permutation(jax.random.fold_in(own_key, 2), number_of)]


def normal_values(own_key, extent, spread, most, shards=(), kind=jnp.bfloat16):
    level = level_of(own_key, extent, shards, -0.22, 0.18) if shards else 1.0
    result = jax.random.normal(own_key, extent, jnp.float32) * spread * level
    return jnp.minimum(jnp.maximum(result, -most), most).astype(kind)


def bell_draw_with(own_key, extent, deviation, bound, shards, heavy, kind=jnp.bfloat16):
    array = deviation * jax.random.normal(own_key, extent, jnp.float32)
    if shards:
        array = array * level_of(own_key, extent, shards, -0.22, 0.18)
    return jnp.clip(spiked(array, jax.random.fold_in(own_key, 3), *heavy), -bound, bound).astype(kind)


def setup_inputs(seed: int = 0) -> dict:
    key_of = jax.random.split(jax.random.key(seed), 16)
    block_input = normal_values(key_of[0], (TOKENS, D), 1.0, 6.0, ((0, 32),), jnp.float32)
    output_cotangent = bell_draw_with(key_of[1], (TOKENS, D), 1.0, 6.0, ((0, 32),), (0, 1, 32, 2.75), jnp.float32)
    sequence_lengths = jax.vmap(lambda own: ragged_sizes(own, SEQS, TOK_DEV, MOST, 2))(jax.random.split(key_of[2], N_DP)).reshape((N_DP, SEQS)).astype(jnp.int32)
    first_gain = jnp.clip(1.0 + 0.1 * jax.random.normal(key_of[3], (D,), jnp.float32), 0.5, 1.5).astype(jnp.bfloat16)
    first_shift = normal_values(key_of[4], (D,), 0.3, 1.796875, ((0, 16),))
    heads_weight = normal_values(key_of[5], (3, D, D), D ** -0.5, 0.1875, ((1, 16), (2, 2)))
    heads_bias = normal_values(key_of[6], (3, D), 0.3, 1.796875, ((1, 32),))
    mixer_weight = normal_values(key_of[7], (D, D), (D // 16) ** -0.5, 0.75, ((0, 2), (1, 16)))
    mixer_bias = normal_values(key_of[8], (D,), 0.3, 1.796875, ((0, 16),))
    second_gain = jnp.clip(1.0 + 0.1 * jax.random.normal(key_of[9], (D,), jnp.float32), 0.5, 1.5).astype(jnp.bfloat16)
    second_shift = normal_values(key_of[10], (D,), 0.3, 1.796875, ((0, 16),))
    widen_weight = normal_values(key_of[11], (D, FF), D ** -0.5, 0.1875, ((0, 16), (1, 2)))
    widen_bias = normal_values(key_of[12], (FF,), 0.3, 1.796875, ((0, 32),))
    narrow_weight = normal_values(key_of[13], (FF, D), FF ** -0.5, 0.09375, ((0, 2), (1, 16)))
    narrow_bias = normal_values(key_of[14], (D,), 0.3, 1.796875, ((0, 16),))
    return {"block_input": block_input, "output_cotangent": output_cotangent, "sequence_lengths": sequence_lengths, "first_gain": first_gain, "first_shift": first_shift, "heads_weight": heads_weight, "heads_bias": heads_bias, "mixer_weight": mixer_weight, "mixer_bias": mixer_bias, "second_gain": second_gain, "second_shift": second_shift, "widen_weight": widen_weight, "widen_bias": widen_bias, "narrow_weight": narrow_weight, "narrow_bias": narrow_bias}


epsilon = 1e-05
gelu_const = 0.7978845608028654

def layer_norm(rows, gain, shift):
    mean = lax.optimization_barrier(jnp.mean(rows, axis=-1, keepdims=True))
    centred = rows - mean
    inverse = lax.rsqrt(lax.optimization_barrier(jnp.mean(centred * centred, axis=-1, keepdims=True)) + epsilon)
    normed = centred * inverse
    return (normed * gain + shift, normed, inverse)

def norm_back(grad_out, normed, inverse, gain):
    scaled = grad_out * gain
    mean_one = lax.optimization_barrier(jnp.mean(scaled, axis=-1, keepdims=True))
    mean_two = lax.optimization_barrier(jnp.mean(scaled * normed, axis=-1, keepdims=True))
    return inverse * (scaled - mean_one - normed * mean_two)

def gelu_parts(pre):
    inner = gelu_const * (pre + 0.044715 * pre * pre * pre)
    tangent = jnp.tanh(inner)
    value = 0.5 * pre * (1.0 + tangent)
    slope = 0.5 * (1.0 + tangent) + 0.5 * pre * (1.0 - tangent * tangent) * gelu_const * (1.0 + 3.0 * 0.044715 * pre * pre)
    return (value, slope)

def visible_mask(lengths, count):
    ends = jnp.cumsum(lengths.astype(jnp.int32))
    places = jnp.arange(count, dtype=jnp.int32)
    segment = lax.optimization_barrier(jnp.sum((places[:, None] >= ends[None, :]).astype(jnp.int32), axis=1))
    return (segment[:, None] == segment[None, :]) & (places[None, :] <= places[:, None])

def score_rows(query, keys, mask):
    scores = jnp.einsum('qhd,khd->hqk', query.astype(jnp.float32), keys.astype(jnp.float32)) * 0.125
    return jnp.where(mask[None], scores, -1e+30)

def attend(query, keys, values, mask):
    scores = score_rows(query, keys, mask)
    highest = lax.optimization_barrier(jnp.max(scores, axis=-1, keepdims=True))
    total = lax.optimization_barrier(jnp.sum(jnp.exp(scores - highest), axis=-1, keepdims=True))
    logsum = highest + jnp.log(total)
    probs = jnp.exp(scores - logsum).astype(jnp.bfloat16)
    attended = jnp.einsum('hqk,khd->qhd', probs.astype(jnp.float32), values.astype(jnp.float32)).astype(jnp.bfloat16)
    return (attended, logsum)

def attend_back(query, keys, values, attended, logsum, grad_att, mask):
    scores = score_rows(query, keys, mask)
    probs = jnp.exp(scores - logsum)
    probs_low = probs.astype(jnp.bfloat16).astype(jnp.float32)
    grad_f = grad_att.astype(jnp.float32)
    grad_values = jnp.einsum('hqk,qhd->khd', probs_low, grad_f)
    grad_probs = jnp.einsum('qhd,khd->hqk', grad_f, values.astype(jnp.float32))
    delta = lax.optimization_barrier(jnp.sum(grad_f * attended.astype(jnp.float32), axis=-1))
    delta = jnp.transpose(delta)[:, :, None]
    grad_scores = (probs * (grad_probs - delta) * 0.125).astype(jnp.bfloat16).astype(jnp.float32)
    grad_query = jnp.einsum('hqk,khd->qhd', grad_scores, keys.astype(jnp.float32))
    grad_keys = jnp.einsum('hqk,qhd->khd', grad_scores, query.astype(jnp.float32))
    return (grad_query, grad_keys, grad_values)

def reference(block_input, output_cotangent, sequence_lengths, first_gain, first_shift, heads_weight, heads_bias, mixer_weight, mixer_bias, second_gain, second_shift, widen_weight, widen_bias, narrow_weight, narrow_bias):
    gain_one = first_gain.astype(jnp.float32)
    shift_one = first_shift.astype(jnp.float32)
    gain_two = second_gain.astype(jnp.float32)
    shift_two = second_shift.astype(jnp.float32)
    hbias = heads_bias.astype(jnp.float32)

    def shard_step(carry, inputs):
        rows, cotangent, lengths = inputs
        mask = visible_mask(lengths, TOK_DEV)
        hidden_one, normed_one, inverse_one = layer_norm(rows, gain_one, shift_one)
        first_act = hidden_one.astype(jnp.bfloat16)
        projected = [(jnp.dot(first_act, heads_weight[j], preferred_element_type=jnp.float32) + hbias[j]).astype(jnp.bfloat16).reshape(TOK_DEV, H, HD) for j in range(3)]
        query, keys, values = projected
        attended, logsum = attend(query, keys, values, mask)
        attended_flat = attended.reshape(TOK_DEV, D)
        middle = rows + jnp.dot(attended_flat, mixer_weight, preferred_element_type=jnp.float32) + mixer_bias.astype(jnp.float32)
        hidden_two, normed_two, inverse_two = layer_norm(middle, gain_two, shift_two)
        second_act = hidden_two.astype(jnp.bfloat16)
        pre = jnp.dot(second_act, widen_weight, preferred_element_type=jnp.float32) + widen_bias.astype(jnp.float32)
        value, slope = gelu_parts(pre)
        hidden = value.astype(jnp.bfloat16)
        output = middle + jnp.dot(hidden, narrow_weight, preferred_element_type=jnp.float32) + narrow_bias.astype(jnp.float32)
        cot_low = cotangent.astype(jnp.bfloat16)
        grad_narrow = jnp.dot(hidden.T, cot_low, preferred_element_type=jnp.float32)
        grad_pre = jnp.dot(cot_low, narrow_weight.T, preferred_element_type=jnp.float32) * slope
        grad_pre_low = grad_pre.astype(jnp.bfloat16)
        grad_widen = jnp.dot(second_act.T, grad_pre_low, preferred_element_type=jnp.float32)
        grad_second = jnp.dot(grad_pre_low, widen_weight.T, preferred_element_type=jnp.float32)
        grad_middle = cotangent + norm_back(grad_second, normed_two, inverse_two, gain_two)
        middle_low = grad_middle.astype(jnp.bfloat16)
        grad_mixer = jnp.dot(attended_flat.T, middle_low, preferred_element_type=jnp.float32)
        grad_att = jnp.dot(middle_low, mixer_weight.T, preferred_element_type=jnp.float32).astype(jnp.bfloat16).reshape(TOK_DEV, H, HD)
        grad_query, grad_keys, grad_values = attend_back(query, keys, values, attended, logsum, grad_att, mask)
        grad_proj = jnp.stack([grad_query, grad_keys, grad_values]).reshape(3, TOK_DEV, D)
        grad_hbias = lax.optimization_barrier(jnp.sum(grad_proj, axis=1))
        proj_low = grad_proj.astype(jnp.bfloat16)
        grad_heads = jnp.stack([jnp.dot(first_act.T, proj_low[j], preferred_element_type=jnp.float32) for j in range(3)])
        grad_first = jnp.dot(proj_low[0], heads_weight[0].T, preferred_element_type=jnp.float32)
        grad_first = grad_first + jnp.dot(proj_low[1], heads_weight[1].T, preferred_element_type=jnp.float32)
        grad_first = grad_first + jnp.dot(proj_low[2], heads_weight[2].T, preferred_element_type=jnp.float32)
        input_grad = grad_middle + norm_back(grad_first, normed_one, inverse_one, gain_one)
        smalls = jnp.stack([lax.optimization_barrier(jnp.sum(grad_first * normed_one, axis=0)), lax.optimization_barrier(jnp.sum(grad_first, axis=0)), lax.optimization_barrier(jnp.sum(grad_middle, axis=0)), lax.optimization_barrier(jnp.sum(grad_second * normed_two, axis=0)), lax.optimization_barrier(jnp.sum(grad_second, axis=0)), lax.optimization_barrier(jnp.sum(cotangent, axis=0))])
        terms = (grad_heads, grad_hbias, grad_mixer, grad_widen, lax.optimization_barrier(jnp.sum(grad_pre, axis=0)), grad_narrow, smalls)
        carry = tuple((a + b for a, b in zip(carry, terms)))
        return (carry, (output, input_grad))
    start = (jnp.zeros((3, D, D), jnp.float32), jnp.zeros((3, D), jnp.float32), jnp.zeros((D, D), jnp.float32), jnp.zeros((D, FF), jnp.float32), jnp.zeros((FF,), jnp.float32), jnp.zeros((FF, D), jnp.float32), jnp.zeros((6, D), jnp.float32))
    inputs = (block_input.reshape(N_DP, TOK_DEV, D), output_cotangent.reshape(N_DP, TOK_DEV, D), sequence_lengths)
    totals, outputs = lax.scan(shard_step, start, inputs)
    block_output = outputs[0].reshape(N_DP * TOK_DEV, D)
    input_gradient = outputs[1].reshape(N_DP * TOK_DEV, D)
    grad_heads, grad_hbias, grad_mixer, grad_widen, grad_wbias, grad_narrow, smalls = totals
    return (block_output, input_gradient, smalls[0], smalls[1], grad_heads, grad_hbias, grad_mixer, smalls[2], smalls[3], smalls[4], grad_widen, grad_wbias, grad_narrow, smalls[5])
```

```python
import jax
import jax.numpy as jnp
from jax import lax
from jax.experimental import pallas as pl
from jax.experimental.pallas import tpu as pltpu
from jax.sharding import PartitionSpec as P


HD = 64
F32 = jnp.float32
BF16 = jnp.bfloat16


epsilon = 1e-05
gelu_const = 0.7978845608028654


def layer_norm(rows, gain, shift):
    mean = jnp.mean(rows, axis=-1, keepdims=True)
    centred = rows - mean
    inverse = lax.rsqrt(jnp.mean(centred * centred, axis=-1, keepdims=True) + epsilon)
    normed = centred * inverse
    return (normed * gain + shift, normed, inverse)


def norm_back(grad_out, normed, inverse, gain):
    scaled = grad_out * gain
    mean_one = jnp.mean(scaled, axis=-1, keepdims=True)
    mean_two = jnp.mean(scaled * normed, axis=-1, keepdims=True)
    return inverse * (scaled - mean_one - normed * mean_two)


def gelu_parts(pre):
    inner = gelu_const * (pre + 0.044715 * pre * pre * pre)
    tangent = jnp.tanh(inner)
    value = 0.5 * pre * (1.0 + tangent)
    slope = 0.5 * (1.0 + tangent) + 0.5 * pre * (1.0 - tangent * tangent) * gelu_const * (
        1.0 + 3.0 * 0.044715 * pre * pre
    )
    return (value, slope)


def dot(a, b, over=((1,), (0,))):
    return lax.dot_general(a, b, (over, ((), ())), preferred_element_type=F32)


ROWS = ((1,), (1,))
COLS = ((0,), (0,))
VMEM = pl.BlockSpec(memory_space=pltpu.VMEM)
SMEM = pl.BlockSpec(memory_space=pltpu.SMEM)
ANY = pl.BlockSpec(memory_space=pl.ANY)
LANES = 128
SMALL = 16


def dp_stages(count):
    factors = []
    rest = count
    tail = []
    if rest % 2 == 0:
        tail = [2]
        rest //= 2
    while rest > 1:
        f = next(k for k in (4, 2, 3, 5, 7, rest) if rest % k == 0)
        factors.append(f)
        rest //= f
    factors += tail
    stages = []
    stride = count
    for f in factors:
        stride //= f
        stages.append((f, stride))
    return stages


def rotation(count, factor, stride, step):
    pairs = []
    for i in range(count):
        place = i // stride % factor
        pairs.append((i, i + ((place + step) % factor - place) * stride))
    return pairs


def send(value, axis, pairs):
    return lax.ppermute(value, axis, pairs)


def kernel(body, outs, ins, specs, scratch=()):
    return pl.pallas_call(
        body,
        out_shape=[jax.ShapeDtypeStruct(shape, dtype) for shape, dtype in outs],
        in_specs=specs,
        out_specs=[VMEM] * len(outs),
        scratch_shapes=list(scratch),
    )(*ins)


class Pieces:
    def __init__(self, buffers, shifts, stages):
        self.buffers, self.shifts, self.stages = buffers, shifts, stages

    def origin(self, index, b, p):
        if not self.shifts[b][p]:
            return 0
        at = 0
        for k, (factor, stride) in zip(self.shifts[b][p], self.stages):
            at = at + lax.rem(index // stride % factor - k + factor, factor) * stride
        return at

    @property
    def total(self):
        return sum(b.shape[0] for b in self.buffers)

    def load(self, refs, into, sems, index):
        copies = []
        for b, ref in enumerate(refs):
            rows = ref.shape[1]
            for p in range(ref.shape[0]):
                at = pl.multiple_of(self.origin(index, b, p) * rows, rows)
                copy = pltpu.make_async_copy(ref.at[p], into.at[pl.ds(at, rows)], sems.at[len(copies)])
                copy.start()
                copies.append(copy)
        return copies


def gather_pieces(block, count, stages):
    held = [(block[None], [()])]
    for factor, stride in stages:
        arrived = []
        for k in range(factor):
            for piece, shifts in held:
                if k:
                    piece = send(piece, "dp", rotation(count, factor, stride, k))
                arrived.append((piece, [s + (k,) for s in shifts]))
        held = arrived
    return Pieces([h for h, _ in held], [s for _, s in held], stages)


def gather_rows(block, index, count, stages):
    rows, cols = block.shape
    held = block[None]
    for factor, stride in stages:
        place = index // stride % factor
        many = held.shape[0]
        whole = jnp.zeros((many, factor, rows, cols), block.dtype)
        for k in range(factor):
            piece = lax.ppermute(held, "dp", rotation(count, factor, stride, k)) if k else held
            source = (place - k + factor) % factor
            whole = lax.dynamic_update_slice(whole, piece[:, None], (0, source, 0, 0))
        held = whole.reshape(many * factor, rows, cols)
    return held.reshape(count * rows, cols)


def split_sum(parts, factor, stride, first=None):
    pieces, rows, cols = parts[0].shape
    many = pieces // factor
    kinds = [first or parts[0].dtype] + [parts[0].dtype] * (factor - 1)

    def body(*refs):
        ins, outs = refs[: len(parts)], refs[len(parts) :]
        place = lax.axis_index("dp") // stride % factor

        def one(m):
            for k, out in enumerate(outs):
                at = m * factor + lax.rem(place + k, factor)
                wide = F32 if len(ins) > 2 else out.dtype
                total = ins[0][at].astype(wide)
                for ref in ins[1:]:
                    total = total + ref[at].astype(wide)
                out[m] = total.astype(out.dtype)

        if many <= 8:
            for m in range(many):
                one(m)
        else:
            lax.fori_loop(0, many, lambda m, c: (one(m), c)[1], 0)

    outs = [((many, rows, cols), kind) for kind in kinds]
    return kernel(body, outs, parts, [VMEM] * len(parts))


def scatter_from(keep, sent, count, stages):
    for at in range(len(stages) - 1, -1, -1):
        factor, stride = stages[at]
        parts = [keep] + [send(s, "dp", rotation(count, factor, stride, k + 1)) for k, s in enumerate(sent)]
        if at == 0:
            return parts
        factor, stride = stages[at - 1]
        keep, *sent = split_sum(parts, factor, stride, F32 if at == 1 else None)


def place_rows(own, other, into, side):
    rows = own.shape[0]
    into[pl.ds(pl.multiple_of(side * rows, rows), rows), :] = own[...].astype(F32)
    into[pl.ds(pl.multiple_of((1 - side) * rows, rows), rows), :] = other[...].astype(F32)


def masks(lengths, rows):
    def segment(places):
        total = jnp.zeros(places.shape, jnp.int32)
        end = 0
        for i in range(lengths.shape[1]):
            end = end + lengths[0, i]
            total = total + (places >= end).astype(jnp.int32)
        return total

    q = lax.broadcasted_iota(jnp.int32, (rows, rows), 0)
    k = lax.broadcasted_iota(jnp.int32, (rows, rows), 1)
    return (segment(q) == segment(k)) & (k <= q)


def shards(
    block_input,
    output_cotangent,
    sequence_lengths,
    first_gain,
    first_shift,
    heads_weight,
    heads_bias,
    mixer_weight,
    mixer_bias,
    second_gain,
    second_shift,
    widen_weight,
    widen_bias,
    narrow_weight,
    narrow_bias,
):
    count = lax.axis_size("dp")
    stages = dp_stages(count)
    index = lax.axis_index("dp")
    side = lax.axis_index("tensor")
    swap = [(0, 1), (1, 0)]
    own, width = block_input.shape
    rows = 2 * own
    block = width // count
    local = heads_weight.shape[2]
    wide = widen_weight.shape[1]
    heads = local // HD
    hcols = 3 * local + local
    across = lambda v: send(v, "tensor", swap)
    direct = block % 16 == 0
    pairs = count // 2

    small_parts = [first_gain, first_shift, mixer_bias, second_gain, second_shift, narrow_bias]
    widen_to = lambda v: jnp.pad(v, ((0, 0), (0, LANES - v.shape[1])))
    smalls = [widen_to(jnp.stack(small_parts)), widen_to(heads_bias), widen_to(widen_bias[None])]
    smalls = jnp.concatenate([*smalls, jnp.zeros((SMALL - 10, LANES), BF16)], axis=0)

    def join_smalls(blocks, r, n):
        return jnp.concatenate([blocks(d, r)[:, :n] for d in range(count)], axis=1)

    head_rows = heads_weight.transpose(1, 0, 2).reshape(block, 3 * local)
    if direct:
        pack = jnp.concatenate(
            [head_rows, mixer_weight.T, jnp.pad(smalls, ((0, block - SMALL), (0, 0)))], axis=1
        )
        hm = gather_pieces(pack, count, stages)
        wp = gather_pieces(widen_weight, count, stages)
        np_ = gather_pieces(narrow_weight.T, count, stages)
        small_source = hm
    else:
        whole = lambda v: Pieces([gather_rows(v, index, count, stages)[None]], [[()]], stages)
        pack = jnp.concatenate([head_rows, mixer_weight.T], axis=1)
        hm, wp, np_ = whole(pack), whole(widen_weight), whole(narrow_weight.T)
        got = gather_rows(smalls, index, count, stages).reshape(count, SMALL, LANES)
        small_source = Pieces([got], [[()] * count], stages)
    pcols = hm.buffers[0].shape[2]

    input_other = across(block_input.astype(BF16))
    cot_other = across(output_cotangent.astype(BF16))

    nh = len(hm.buffers)
    extra = [] if direct else small_source.buffers

    def forward_one(len_ref, own_ref, other_ref, *refs):
        h_refs, refs = refs[:nh], refs[nh:]
        e_refs, refs = refs[: len(extra)], refs[len(extra) :]
        act_ref, proj_ref, att_ref, lse_ref, mixed_ref, base_ref, vec_ref, wb_ref, w, xf, sems = refs
        copies = hm.load(h_refs, w, sems, lax.axis_index("dp"))
        place_rows(own_ref, other_ref, xf, lax.axis_index("tensor"))
        for copy in copies:
            copy.wait()
        if direct:
            blocks = lambda d, r: w[d * block : d * block + SMALL, hcols:pcols].astype(F32)[r : r + 1]
        else:
            blocks = lambda d, r: e_refs[0][d].astype(F32)[r : r + 1]
        vectors = [join_smalls(blocks, r, block) for r in range(6)]
        for r in range(6):
            vec_ref[r : r + 1, :] = vectors[r]
        hbias = jnp.concatenate([join_smalls(blocks, 6 + j, local // count) for j in range(3)], axis=1)
        wb_ref[...] = join_smalls(blocks, 9, wide // count)
        hidden, _, _ = layer_norm(xf[...], vectors[0], vectors[1])
        act = hidden.astype(BF16)
        act_ref[...] = act
        proj_ref[...] = (dot(act, w[:, : 3 * local]) + hbias).astype(BF16)
        mask = masks(len_ref, rows)
        lanes = lax.broadcasted_iota(jnp.int32, (rows, LANES), 1)
        lse_all = jnp.zeros((rows, LANES), F32)
        per = LANES // HD
        for first in range(0, heads, per):
            outs = []
            for h in range(first, first + per):
                q = proj_ref[:, h * HD : (h + 1) * HD]
                k = proj_ref[:, local + h * HD : local + (h + 1) * HD]
                v = proj_ref[:, 2 * local + h * HD : 2 * local + (h + 1) * HD]
                scores = jnp.where(mask, dot(q, k, ROWS) * 0.125, -1e30)
                highest = jnp.max(scores, axis=-1, keepdims=True)
                powers = jnp.exp(scores - highest)
                total = jnp.sum(powers, axis=-1, keepdims=True)
                outs.append(dot((powers * (1.0 / total)).astype(BF16), v))
                lse_all = jnp.where(lanes == h, highest + jnp.log(total), lse_all)
            att_ref[:, first * HD : (first + per) * HD] = jnp.concatenate(outs, axis=1).astype(BF16)
        lse_ref[...] = lse_all
        mixed = dot(att_ref[...], w[:, 3 * local : hcols], ROWS)
        mixed_ref[...] = mixed.astype(BF16)
        base_ref[...] = xf[...] + mixed + vectors[2]

    sem = lambda p: pltpu.SemaphoreType.DMA((p.total,))
    act, proj, att, lse, mixed, base, vectors, wbias = kernel(
        forward_one,
        [
            ((rows, width), BF16),
            ((rows, 3 * local), BF16),
            ((rows, local), BF16),
            ((rows, LANES), F32),
            ((rows, width), BF16),
            ((rows, width), F32),
            ((8, width), F32),
            ((1, wide), F32),
        ],
        [sequence_lengths, block_input, input_other, *hm.buffers, *extra],
        [SMEM, VMEM, VMEM] + [ANY] * nh + [VMEM] * len(extra),
        [pltpu.VMEM((width, pcols), BF16), pltpu.VMEM((rows, width), F32), sem(hm)],
    )
    mixed_other = across(mixed)

    nw = len(wp.buffers)
    nn = len(np_.buffers)
    halves = [((width // (2 if direct else 1), wide), BF16)] * (2 if direct else 1)

    def write_left(value, kept, left):
        turned = value.T.astype(BF16)
        if not direct:
            kept[...] = turned
            return
        core = lax.axis_index("dp") % 2
        for m in range(pairs):
            low = turned[m * 2 * block : (m * 2 + 1) * block]
            high = turned[(m * 2 + 1) * block : (m * 2 + 2) * block]
            kept[m * block : (m + 1) * block] = jnp.where(core == 0, low, high)
            left[m * block : (m + 1) * block] = jnp.where(core == 0, high, low)

    def write_grad(lefts, right, groups, each, at=0):
        total = right.shape[1]
        step = min(total, 512)
        for c in range(0, total, step):
            outs = groups[(at + c) // each]
            cut = slice((at + c) % each, (at + c) % each + step)
            for left, out in zip(lefts, outs):
                out[:, cut] = dot(left[...], right[:, c : c + step]).astype(BF16)

    sides = 2 if direct else 1
    left_shape = (width // sides, rows)

    def forward_two(base_ref, other_ref, vec_ref, wb_ref, cot_ref, coto_ref, *refs):
        w_refs, refs = refs[:nw], refs[nw:]
        mid_ref, act_ref, hid_ref, slope_ref, cotb_ref, *lefts, w, sems = refs
        copies = wp.load(w_refs, w, sems, lax.axis_index("dp"))
        place_rows(cot_ref, coto_ref, mid_ref, lax.axis_index("tensor"))
        cotb_ref[...] = mid_ref[...].astype(BF16)
        write_left(mid_ref[...], lefts[0], lefts[-1])
        middle = base_ref[...] + other_ref[...].astype(F32)
        mid_ref[...] = middle
        hidden, _, _ = layer_norm(middle, vec_ref[3:4, :], vec_ref[4:5, :])
        act_ref[...] = hidden.astype(BF16)
        for copy in copies:
            copy.wait()
        step = min(wide, 512)
        for c in range(0, wide, step):
            pre = dot(act_ref[...], w[:, c : c + step]) + wb_ref[:, c : c + step]
            value, slope = gelu_parts(pre)
            hid_ref[:, c : c + step] = value.astype(BF16)
            slope_ref[:, c : c + step] = slope

    middle, act2, hidden, slope, cotb, *cot_left = kernel(
        forward_two,
        [
            ((rows, width), F32),
            ((rows, width), BF16),
            ((rows, wide), BF16),
            ((rows, wide), F32),
            ((rows, width), BF16),
            *[(left_shape, BF16)] * sides,
        ],
        [base, mixed_other, vectors, wbias, output_cotangent, cot_other, *wp.buffers],
        [VMEM] * 6 + [ANY] * nw,
        [pltpu.VMEM((width, wide), BF16), sem(wp)],
    )

    def narrow_grad(*refs):
        lefts, right, outs = refs[:sides], refs[sides], refs[sides + 1 :]
        write_grad(lefts, right, [outs], wide)

    grad_narrow = kernel(narrow_grad, halves, [*cot_left, hidden], [VMEM] * (sides + 1))

    def turn(act_ref, act2_ref, *outs):
        write_left(act_ref[...].astype(F32), outs[0], outs[sides - 1])
        write_left(act2_ref[...].astype(F32), outs[sides], outs[2 * sides - 1])

    turned = kernel(turn, [(left_shape, BF16)] * (2 * sides), [act, act2], [VMEM] * 2)
    act_left, act2_left = turned[:sides], turned[sides:]

    def scatter(parts):
        factor, stride = stages[-1]
        if not direct:
            parts = split_sum([parts[0].reshape(count, block, -1)], factor, stride)
        parts = [p.reshape(-1, block, p.shape[-1]) for p in parts]
        return scatter_from(parts[0], parts[1:], count, stages)

    def added(refs):
        total = refs[0][0]
        for ref in refs[1:]:
            total = total + ref[0].astype(F32)
        return total

    def final(parts):
        def add(*refs):
            refs[-1][...] = added(refs[:-1])

        return kernel(add, [(parts[0].shape[1:], F32)], parts, [VMEM] * len(parts))[0]

    narrow_out = final(scatter(grad_narrow)).T

    def backward_three(cot_ref, slope_ref, *refs):
        n_refs, (gp_ref, wb_ref, n, sems) = refs[:nn], refs[nn:]
        for copy in np_.load(n_refs, n, sems, lax.axis_index("dp")):
            copy.wait()
        step = min(wide, 512)
        for c in range(0, wide, step):
            grad = dot(cot_ref[...], n[:, c : c + step]) * slope_ref[:, c : c + step]
            wb_ref[:, c : c + step] = jnp.sum(grad, axis=0, keepdims=True)
            gp_ref[:, c : c + step] = grad.astype(BF16)

    grad_pre, grad_wbias = kernel(
        backward_three,
        [((rows, wide), BF16), ((1, wide), F32)],
        [cotb, slope, *np_.buffers],
        [VMEM] * 2 + [ANY] * nn,
        [pltpu.VMEM((width, wide), BF16), sem(np_)],
    )

    def second_back(gp_ref, *refs):
        w_refs, (sec_ref, low_ref, w, sems) = refs[:nw], refs[nw:]
        for copy in wp.load(w_refs, w, sems, lax.axis_index("dp")):
            copy.wait()
        part = dot(gp_ref[...], w[...], ROWS)
        sec_ref[...] = part
        low_ref[...] = part.astype(BF16)

    second, second_low = kernel(
        second_back,
        [((rows, width), F32), ((rows, width), BF16)],
        [grad_pre, *wp.buffers],
        [VMEM] + [ANY] * nw,
        [pltpu.VMEM((width, wide), BF16), sem(wp)],
    )
    second_other = across(second_low)

    def widen_grad(*refs):
        lefts, right, outs = refs[:sides], refs[sides], refs[sides + 1 :]
        write_grad(lefts, right, [outs], wide)

    grad_widen = kernel(widen_grad, halves, [*act2_left, grad_pre], [VMEM] * (sides + 1))
    widen_out = final(scatter(grad_widen))

    def narrow_forward(hid_ref, mid_ref, vec_ref, *refs):
        n_refs, refs = refs[:nn], refs[nn:]
        out_ref, low_ref, n, full, sems = refs
        for copy in np_.load(n_refs, n, sems, lax.axis_index("dp")):
            copy.wait()
        full[...] = dot(hid_ref[...], n[...], ROWS)
        me = lax.axis_index("tensor")
        mine = pl.ds(pl.multiple_of(me * own, own), own)
        theirs = pl.ds(pl.multiple_of((1 - me) * own, own), own)
        out_ref[...] = full[mine, :] + mid_ref[mine, :] + vec_ref[5:6, :]
        low_ref[...] = full[theirs, :].astype(BF16)

    ffn_own, ffn_low = kernel(
        narrow_forward,
        [((own, width), F32), ((own, width), BF16)],
        [hidden, middle, vectors, *np_.buffers],
        [VMEM] * 3 + [ANY] * nn,
        [pltpu.VMEM((width, wide), BF16), pltpu.VMEM((rows, width), F32), sem(np_)],
    )
    block_output = ffn_own + across(ffn_low).astype(F32)

    hcut = hcols // 2
    hhalves = [((width // sides, hcut + (LANES if direct else 0)), BF16)] * sides
    hhalves += [((width // sides, hcut), BF16)] * sides
    if not direct:
        hhalves.append(((count, SMALL, LANES), F32))

    def tail_of(vectors, hbias, wbias, d):
        part = local // count
        each = wide // count
        at = d * block // LANES * LANES
        out = [v[:, at : at + LANES] for v in vectors]
        at = d * part // LANES * LANES
        out += [hbias[:, j * local + at : j * local + at + LANES] for j in range(3)]
        at = d * each // LANES * LANES
        out += [wbias[:, at : at + LANES], jnp.zeros((SMALL - 10, LANES), F32)]
        return jnp.concatenate(out, axis=0)

    def backward_four(sec_ref, other_ref, mid_ref, vec_ref, cot_ref, coto_ref, proj_ref, att_ref, *refs):
        lse_ref, x_ref, xo_ref, wb_ref, len_ref, *refs = refs
        act_lefts, refs = refs[:sides], refs[sides:]
        h_refs, refs = refs[:nh], refs[nh:]
        gm_ref, part_ref, low_ref, *outs, w, cf, gatt, midb, pb_ref, hb_ref, left_a, left_b, sems = refs
        copies = hm.load(h_refs, w, sems, lax.axis_index("dp"))
        me = lax.axis_index("tensor")
        mine = pl.ds(pl.multiple_of(me * own, own), own)
        theirs = pl.ds(pl.multiple_of((1 - me) * own, own), own)
        place_rows(cot_ref, coto_ref, cf, me)
        column = lambda v: jnp.sum(v, axis=0, keepdims=True)
        grad = sec_ref[...] + other_ref[...].astype(F32)
        _, normed, inverse = layer_norm(mid_ref[...], vec_ref[3:4, :], vec_ref[4:5, :])
        vectors = [column(grad * normed), column(grad), column(cf[...])]
        middle_grad = cf[...] + norm_back(grad, normed, inverse, vec_ref[3:4, :])
        cf[...] = middle_grad
        vectors = [column(middle_grad), *vectors]
        gm_ref[...] = cf[mine, :]
        midb[...] = middle_grad.astype(BF16)
        for copy in copies:
            copy.wait()
        gatt[...] = dot(midb[...], w[:, 3 * local : hcols]).astype(BF16)
        mask = masks(len_ref, rows)
        per = LANES // HD
        for first in range(0, heads, per):
            parts = [[], [], []]
            for h in range(first, first + per):
                at = slice(h * HD, (h + 1) * HD)
                q = proj_ref[:, at]
                k = proj_ref[:, local + h * HD : local + (h + 1) * HD]
                v = proj_ref[:, 2 * local + h * HD : 2 * local + (h + 1) * HD]
                g = gatt[:, at]
                delta = jnp.sum(g.astype(F32) * att_ref[:, at].astype(F32), axis=-1, keepdims=True)
                scores = jnp.where(mask, dot(q, k, ROWS) * 0.125, -1e30)
                probs = jnp.exp(scores - lse_ref[:, h : h + 1])
                grad_scores = (probs * (dot(g, v, ROWS) - delta) * 0.125).astype(BF16)
                parts[0].append(dot(grad_scores, k))
                parts[1].append(dot(grad_scores, q, COLS))
                parts[2].append(dot(probs.astype(BF16), g, COLS))
            for j in range(3):
                joined = jnp.concatenate(parts[j], axis=1)
                at = slice(j * local + first * HD, j * local + (first + per) * HD)
                hb_ref[:, at] = column(joined)
                pb_ref[:, at] = joined.astype(BF16)
        groups = [outs[:sides], outs[sides : 2 * sides]]
        write_left(cf[...], left_a, left_b)
        part = dot(pb_ref[...], w[:, : 3 * local], ROWS)
        place_rows(x_ref, xo_ref, cf, me)
        _, normed, _ = layer_norm(cf[...], vec_ref[0:1, :], vec_ref[1:2, :])
        vectors = [column(part * normed), column(part), *vectors]
        cf[...] = part
        part_ref[...] = cf[mine, :]
        low_ref[...] = cf[theirs, :].astype(BF16)
        write_grad([left_a, left_b][:sides], att_ref, groups, hcut, 3 * local)
        write_grad(act_lefts, pb_ref, groups, hcut)
        tail = lambda d: tail_of(vectors, hb_ref[...], wb_ref[...], d)
        if not direct:
            for d in range(count):
                outs[2 * sides][d] = tail(d)
            return
        core = lax.axis_index("dp") % 2
        for m in range(pairs):
            low, high = tail(2 * m), tail(2 * m + 1)
            for out, value in zip(groups[0], (jnp.where(core == 0, low, high), jnp.where(core == 0, high, low))):
                out[m * block : m * block + SMALL, hcut:] = value.astype(BF16)
                out[m * block + SMALL : (m + 1) * block, hcut:] = jnp.zeros((block - SMALL, LANES), BF16)

    grad_mid, first_part, first_low, *grad_heads = kernel(
        backward_four,
        [((own, width), F32), ((own, width), F32), ((own, width), BF16), *hhalves],
        [second, second_other, middle, vectors, output_cotangent, cot_other, proj, att, lse]
        + [block_input, input_other, grad_wbias, sequence_lengths, *act_left, *hm.buffers],
        [VMEM] * 12 + [SMEM] + [VMEM] * sides + [ANY] * nh,
        [
            pltpu.VMEM((width, pcols), BF16),
            pltpu.VMEM((rows, width), F32),
            pltpu.VMEM((rows, local), BF16),
            pltpu.VMEM((rows, width), BF16),
            pltpu.VMEM((rows, 3 * local), BF16),
            pltpu.VMEM((1, 3 * local), F32),
            pltpu.VMEM(left_shape, BF16),
            pltpu.VMEM(left_shape, BF16),
            sem(hm),
        ],
    )
    part_a = scatter(grad_heads[:sides])
    part_b = scatter(grad_heads[sides : 2 * sides])

    def heads_sum(*refs):
        a_refs, b_refs = refs[: len(part_a)], refs[len(part_a) : -2]
        heads_ref, mixer_ref = refs[-2:]
        total_a, total_b = added(a_refs), added(b_refs)
        heads_ref[0] = total_a[:, :local]
        heads_ref[1] = total_a[:, local:hcut]
        heads_ref[2] = total_b[:, :local]
        mixer_ref[...] = total_b[:, local:]

    heads_out, mixer_out = kernel(
        heads_sum,
        [((3, block, local), F32), ((block, local), F32)],
        [*part_a, *part_b],
        [VMEM] * (len(part_a) + len(part_b)),
    )
    mixer_out = mixer_out.T
    first_other = across(first_low)

    def last(part_ref, other_ref, x_ref, gm_ref, vec_ref, out_ref):
        grad = part_ref[...] + other_ref[...].astype(F32)
        _, normed, inverse = layer_norm(x_ref[...], vec_ref[0:1, :], vec_ref[1:2, :])
        out_ref[...] = gm_ref[...] + norm_back(grad, normed, inverse, vec_ref[0:1, :])

    input_gradient = kernel(
        last, [((own, width), F32)], [first_part, first_other, block_input, grad_mid, vectors], [VMEM] * 5
    )[0]
    if direct:

        def tail_sum(*refs):
            refs[-1][...] = added(refs[:-1])

        corner = pl.BlockSpec((1, SMALL, LANES), lambda i: (0, 0, hcut // LANES))
        tails = pl.pallas_call(
            tail_sum,
            grid=(1,),
            out_shape=jax.ShapeDtypeStruct((SMALL, LANES), F32),
            in_specs=[corner] * len(part_a),
            out_specs=pl.BlockSpec((SMALL, LANES), lambda i: (0, 0)),
        )(*part_a)
    else:
        factor, stride = stages[-1]
        keep, *sent = split_sum([grad_heads[2 * sides]], factor, stride)
        tails = sum(scatter_from(keep, sent, count, stages))[0]
    tails = jnp.concatenate([tails[:2] + across(tails[:2]), tails[2:]], axis=0)

    half = block // 2
    part = local // count
    each = wide // count
    pick = lambda r, many, n, at: lax.dynamic_slice(tails, (r, at % LANES), (many, n))
    six = pick(0, 6, half, index * block + side * half)
    hbias_out = pick(6, 3, part, index * part)
    wbias_out = pick(9, 1, each, index * each)[0]
    return (
        block_output,
        input_gradient,
        six[0],
        six[1],
        heads_out,
        hbias_out,
        mixer_out,
        six[2],
        six[3],
        six[4],
        widen_out,
        wbias_out,
        narrow_out,
        six[5],
    )


def solution(mesh):
    in_specs = (
        P(("dp", "tensor"), None),
        P(("dp", "tensor"), None),
        P("dp", None),
        P("dp"),
        P("dp"),
        P(None, "dp", "tensor"),
        P(None, ("tensor", "dp")),
        P("tensor", "dp"),
        P("dp"),
        P("dp"),
        P("dp"),
        P("dp", "tensor"),
        P(("tensor", "dp")),
        P("tensor", "dp"),
        P("dp"),
    )
    out_specs = (
        P(("dp", "tensor"), None),
        P(("dp", "tensor"), None),
        P(("dp", "tensor")),
        P(("dp", "tensor")),
        P(None, "dp", "tensor"),
        P(None, ("tensor", "dp")),
        P("tensor", "dp"),
        P(("dp", "tensor")),
        P(("dp", "tensor")),
        P(("dp", "tensor")),
        P("dp", "tensor"),
        P(("tensor", "dp")),
        P("tensor", "dp"),
        P(("dp", "tensor")),
    )

    return jax.shard_map(shards, mesh=mesh, in_specs=in_specs, out_specs=out_specs, check_vma=False)
```
